512 devices in a mesh: dp: 16 (over x, z_lo), space: 32 (over z_hi, y, core).
Axes of the slice: x: 4, y: 8, z: 8 (z_hi: 2, z_lo: 4; z = z_hi * 4 + z_lo), core: 2. Of those that a mesh axis runs over, the one named last changes fastest.
Arguments:
- field_tiles: bfloat16 [16, 32, 8, 16, 1024], P('dp', 'space'), may hold values from -6 to 6
- mid_weight: bfloat16 [1728, 128], replicated, may hold values from -0.15625 to 0.15625
- deep_weight: bfloat16 [3456, 256], P(None, 'space'), may hold values from -0.109375 to 0.109375
- latent_cotangent: bfloat16 [16, 256, 1024], P('dp', 'space'), may hold values from -6 to 6
Outputs:
- latent: bfloat16 [16, 256, 1024], P('dp', 'space')
- grad_tiles: bfloat16 [16, 32, 8, 16, 1024], P('dp', 'space')
- grad_deep: float32 [3456, 256], P(None, 'space')
The draws below stay inside these ranges and needn't reach their ends.
All inputs are finite; a program needn't handle non-finite values.
Results may differ from the reference program's by a relative error of at most 0.0049.
Values may be sent and summed in bfloat16 or wider, within the bound.
No kernel may reach another device: no remote copies, remote signals or barrier semaphores. Data moves between devices by JAX's collectives and lax.ppermute only.
A program may use at most 64 MiB of HBM per device.

```python
import math
import jax
import jax.numpy as jnp
from jax import lax

C_IN = 64
C_MID = 128
C_OUT = 256
TILE_X = 8
TILE_Y = 16
DEPTH = 16
GRID_Y = 4
GRID_X = 8
SAMPLES = 16
LAT_CELLS = 1024
N_SPACE = 32


def raised(result, stream_key, source, target, blocks, factor):
    owner, partner = [(jnp.arange(result.shape[position]) // (result.shape[position] // blocks)).reshape([-1 if axis == position else 1 for axis in range(result.ndim)]) for position in (source, target)]
    chosen = jax.random.permutation(stream_key, blocks)[partner]
    strong = (owner == chosen) | (owner == (partner + blocks // 2) % blocks)
    return jnp.where(strong, factor * result, result)


def block_scale(own_key, dims, pieces, low, largest):
    level, own = 1.0, jax.random.fold_in(own_key, 6)
    for axis_at, blocks in pieces:
        heights = jnp.exp(jax.random.uniform(jax.random.fold_in(own, axis_at), (blocks,), jnp.float32, low / len(pieces), largest / len(pieces)))
        level = level * jnp.repeat(heights, dims[axis_at] // blocks).reshape([-1 if axis == axis_at else 1 for axis in range(len(dims))])
    return level


def scatter_about(own_key, dims, width, reach, cuts=(), dtype=jnp.bfloat16):
    result = jax.random.normal(own_key, dims, jnp.float32) * width
    if len(cuts) > 0:
        result = block_scale(own_key, dims, cuts, -0.22, 0.18) * result
    return jnp.clip(result, min=-reach, max=reach).astype(dtype)


def noise_with(rng, dims, deviation, limit, pieces, heavy, kind=jnp.bfloat16):
    array = deviation * jax.random.normal(rng, dims, jnp.float32)
    if pieces:
        array = array * block_scale(rng, dims, pieces, -0.22, 0.18)
    return jnp.clip(raised(array, jax.random.fold_in(rng, 3), *heavy), -limit, limit).astype(kind)


def setup_inputs(seed: int = 0) -> dict:
    streams_of = jax.random.split(jax.random.key(seed), 5)
    return {
        "field_tiles": scatter_about(streams_of[0], (SAMPLES, N_SPACE, TILE_X, TILE_Y, DEPTH * C_IN), 1.0, 6.0, ((0, 16), (1, 32))),
        "mid_weight": scatter_about(streams_of[1], (27 * C_IN, C_MID), (27 * C_IN) ** -0.5, 0.15625),
        "deep_weight": scatter_about(streams_of[2], (27 * C_MID, C_OUT), (27 * C_MID) ** -0.5, 0.109375, ((1, 32),)),
        "latent_cotangent": noise_with(streams_of[3], (SAMPLES, C_OUT, LAT_CELLS), 1.0, 6.0, ((0, 16), (1, 32)), (2, 1, 32, 2.75)),
    }


conv_layout = ('NDHWC', 'DHWIO', 'NDHWC')

def conv_mixed(field, kernel):
    return lax.conv_general_dilated(field[None], kernel, (2, 2, 2), ((1, 1), (1, 1), (1, 1)), dimension_numbers=conv_layout, preferred_element_type=jnp.float32)[0]

def conv_exact(field, kernel):
    return lax.conv_general_dilated(field[None], kernel, (2, 2, 2), ((1, 1), (1, 1), (1, 1)), dimension_numbers=conv_layout, precision=lax.Precision.HIGHEST)[0]

def to_slab(tiles_one, cells_x, cells_y, channels):
    shaped = tiles_one.reshape(GRID_X, GRID_Y, cells_x, cells_y, -1, channels)
    shaped = jnp.transpose(shaped, (0, 2, 1, 3, 4, 5))
    return shaped.reshape(GRID_X * cells_x, GRID_Y * cells_y, -1, channels)

def from_slab(slab, cells_x, cells_y):
    channels = slab.shape[3]
    shaped = slab.reshape(GRID_X, cells_x, GRID_Y, cells_y, slab.shape[2], channels)
    shaped = jnp.transpose(shaped, (0, 2, 1, 3, 4, 5))
    return shaped.reshape(N_SPACE, cells_x, cells_y, slab.shape[2] * channels)

def reference(field_tiles, mid_weight, deep_weight, latent_cotangent):
    kern_mid = mid_weight.reshape(3, 3, 3, C_IN, C_MID)
    kern_deep = deep_weight.reshape(3, 3, 3, C_MID, C_OUT)
    quart_x = TILE_X // 4
    quart_y = TILE_Y // 4
    quart_z = DEPTH // 4

    def one_sample(total, paired):
        tiles_one, cot_one = paired
        slab = to_slab(tiles_one, TILE_X, TILE_Y, C_IN)
        pre_act = conv_mixed(slab, kern_mid)
        hidden = jax.nn.silu(pre_act).astype(jnp.bfloat16)
        deep_field = conv_mixed(hidden, kern_deep).astype(jnp.bfloat16)
        latent_one = from_slab(deep_field, quart_x, quart_y).reshape(N_SPACE * quart_x * quart_y * quart_z, C_OUT).T
        cot_field = to_slab(cot_one.T, quart_x, quart_y, C_OUT).astype(jnp.float32)
        _, pull_deep = jax.vjp(conv_exact, hidden.astype(jnp.float32), kern_deep.astype(jnp.float32))
        back_hidden, grad_kernel = pull_deep(cot_field)
        gate_sig = jax.nn.sigmoid(pre_act)
        back_pre = (back_hidden * gate_sig * (1.0 + pre_act * (1.0 - gate_sig))).astype(jnp.bfloat16)
        kern_mid_wide = kern_mid.astype(jnp.float32)
        _, pull_mid = jax.vjp(lambda values: conv_exact(values, kern_mid_wide), slab.astype(jnp.float32))
        back_field, = pull_mid(back_pre.astype(jnp.float32))
        grad_one = from_slab(back_field.astype(jnp.bfloat16), TILE_X, TILE_Y)
        return (total + grad_kernel.reshape(27 * C_MID, C_OUT), (latent_one, grad_one))
    start_total = jnp.zeros((27 * C_MID, C_OUT), jnp.float32)
    total, outputs = lax.scan(one_sample, start_total, (field_tiles, latent_cotangent))
    latent, grad_tiles = outputs
    grad_deep = total * (1.0 / math.sqrt(SAMPLES * LAT_CELLS))
    return (latent, grad_tiles, grad_deep)
```

```python
import itertools
import math

import jax
import jax.numpy as jnp
from jax import lax
from jax.experimental import pallas as pl
from jax.experimental.pallas import tpu as pltpu
from jax.sharding import Mesh, PartitionSpec as P

BF = jnp.bfloat16
F32 = jnp.float32
SPACE = ("zh", "y", "c")
BITS = list(itertools.product((0, 1), repeat=3))
NT = (((1,), (1,)), ((), ()))


def tap_of(parity, shift):
    tap = 0
    for p, s in zip(parity, shift):
        if s > p:
            return None
        tap = tap * 3 + (1 if p == 0 else (0 if s else 2))
    return tap


def call(kernel, out_shape, scratch, args, name):
    return pl.pallas_call(
        kernel,
        out_shape=out_shape,
        in_specs=[pl.BlockSpec(memory_space=pltpu.VMEM)] * len(args),
        out_specs=jax.tree.map(lambda _: pl.BlockSpec(memory_space=pltpu.VMEM), out_shape),
        scratch_shapes=scratch,
        compiler_params=pltpu.CompilerParams(vmem_limit_bytes=40 << 20),
        name=name,
    )(*args)


def shape(dims, dtype):
    return jax.ShapeDtypeStruct(dims, dtype)


def cells_order(rows_first):
    fine = lax.broadcasted_iota(jnp.int32, (256, 256), 0 if rows_first else 1)
    flat = lax.broadcasted_iota(jnp.int32, (256, 256), 1 if rows_first else 0)
    px, py, pz = fine // 128, (fine // 64) % 2, (fine // 32) % 2
    hx, hy, hz = (fine // 16) % 2, (fine // 4) % 4, fine % 4
    return (2 * hz + pz) * 32 + (2 * hx + px) * 8 + 2 * hy + py == flat


def spread_kernel(wc_ref, back_ref, cot_ref, wide_ref, shifted, tiles, weights):
    half, core = lax.axis_index("zh"), lax.axis_index("c")
    cot = wc_ref[:, 3456:].astype(F32)
    lane = lax.broadcasted_iota(jnp.int32, cot.shape, 1)

    def ahead(v, by):
        return pltpu.roll(v, 1024 - by, 1)

    def shift_z(v):
        return jnp.where(lane % 4 < 3, ahead(v, 1), 0.0)

    def shift_y(v):
        inner = (lane // 4) % 4 < 3
        edge = jnp.where((lane // 32) % 4 < 3, ahead(v, 20), 0.0)
        return jnp.where(inner, ahead(v, 4), edge)

    def shift_x(v):
        inner = (lane // 16) % 2 == 0
        edge = jnp.where(lane // 128 < 7, ahead(v, 112), 0.0)
        return jnp.where(inner, ahead(v, 16), edge)

    for n, (sx, sy, sz) in enumerate(BITS):
        v = cot
        if sz:
            v = shift_z(v)
        if sy:
            v = shift_y(v)
        if sx:
            v = shift_x(v)
        shifted[n * 32 : (n + 1) * 32, :] = v
    mine = shifted[:, pl.ds(pl.multiple_of(half * 512, 512), 512)]
    tiles[...] = mine.T.reshape(16, 32, 256)
    picked = jnp.concatenate([tiles[2 * y + core] for y in range(8)], axis=0).astype(BF)
    zero = jnp.zeros((32, 128), BF)
    for n, s in enumerate(BITS):
        blocks = []
        for p in BITS:
            tap = tap_of(p, s)
            blocks.append(zero if tap is None else wc_ref[:, tap * 128 : (tap + 1) * 128])
        weights[n] = jnp.concatenate(blocks, axis=1)
    wide = weights[...].reshape(256, 1024)
    back = jnp.dot(picked, wide, preferred_element_type=F32).astype(BF)
    back_ref[...] = back.reshape(8, 32, 1024)
    row = pl.multiple_of(core * 16, 16)
    for n in range(8):
        wide_ref[n * 16 : (n + 1) * 16, :] = weights[n, pl.ds(row, 16), :]
        part = shifted[pl.ds(pl.multiple_of(n * 32 + core * 16, 16), 16), :]
        cot_ref[n * 16 : (n + 1) * 16, :] = jnp.where(half == 0, part[:, :512], part[:, 512:]).astype(BF)


def first_kernel(field_ref, from_x_ref, from_y_ref, w_ref, back_ref, pre_ref, send_ref, cells, weights):
    cells[:, 0] = jnp.zeros((9, 32, 128), F32)
    for z in range(8):
        lanes = slice(z * 128, (z + 1) * 128)
        cells[0, z + 1, 8:24, :] = from_x_ref[:, lanes].astype(F32)
        cells[1:9, z + 1, 8:24, :] = field_ref[:, :, lanes].astype(F32)
        from_y = from_y_ref[:, lanes].astype(F32)
        for i in range(9):
            cells[i, z + 1, 7:8, :] = from_y[i : i + 1]
    for n in range(9):
        weights[n * 256 : n * 256 + 64, :] = jnp.zeros((64, 128), BF)
        weights[n * 256 + 64 : (n + 1) * 256, :] = w_ref[n * 192 : (n + 1) * 192, :]
    pre = jnp.zeros((256, 128), F32)
    for a in range(3):
        for b in range(3):
            rows = [
                jnp.concatenate(
                    [cells[2 * ox + a, z, pl.ds(7 + b, 8, stride=2), :] for ox in range(4)], axis=0
                )
                for z in range(9)
            ]
            lower, upper = (jnp.concatenate(rows[i : i + 8], axis=0) for i in range(2))
            patch = jnp.concatenate([lower, upper], axis=1).astype(BF)
            n = a * 3 + b
            pre += jnp.dot(patch, weights[n * 256 : (n + 1) * 256, :], preferred_element_type=F32)
    order = cells_order(True).astype(F32)
    pre = jnp.dot(order, pre, precision=lax.Precision.HIGHEST, preferred_element_type=F32)
    pre_ref[...] = pre
    hidden = (pre * (1.0 / (1.0 + jnp.exp(-pre)))).astype(BF)
    hidden = jnp.concatenate([hidden[n * 32 : (n + 1) * 32] for n in range(8)], axis=1)
    for y in range(8):
        send_ref[y, 0:32, :] = hidden
        send_ref[y, 32:64, :] = back_ref[y]


def back_kernel(got_ref, pre_ref, back_ref, face_x_ref, face_y_ref, rows):
    total = got_ref[0, 32:64, :].astype(F32)
    for y in range(1, 8):
        total += got_ref[y, 32:64, :].astype(F32)
    total = jnp.concatenate([total[:, n * 128 : (n + 1) * 128] for n in range(8)], axis=0)
    pre = pre_ref[...]
    gate = 1.0 / (1.0 + jnp.exp(-pre))
    back = (total * gate * (1.0 + pre * (1.0 - gate))).astype(BF)
    order = cells_order(False).astype(F32).astype(BF)
    back = jnp.dot(order, back, preferred_element_type=F32)
    rows[...] = back
    back_ref[...] = back.astype(BF)
    face_x_ref[...] = jnp.concatenate([back[z * 32 : z * 32 + 8] for z in range(8)], axis=0).astype(BF)
    face_y_ref[...] = rows[pl.ds(0, 32, stride=8), :].astype(BF)


def field_kernel(back_ref, from_x_ref, from_y_ref, w_ref, out_ref, weights, cells):
    own = back_ref[...].astype(F32).reshape(8, 4, 8, 128)
    flat = jnp.concatenate([own, from_x_ref[...].astype(F32).reshape(8, 1, 8, 128)], axis=1)
    edge = from_y_ref[...].astype(F32).reshape(40, 1, 128)
    moved = pltpu.roll(flat.reshape(40, 8, 128), 7, 1)
    last = lax.broadcasted_iota(jnp.int32, (40, 8, 128), 1) == 7
    moved = jnp.where(last, jnp.broadcast_to(edge, (40, 8, 128)), moved).reshape(8, 5, 8, 128)
    none = jnp.zeros((1, 5, 8, 128), F32)
    parts = []
    for sx, sy, sz in BITS:
        v = moved if sy else flat
        if sz:
            v = jnp.concatenate([v[1:], none], axis=0)
        parts.append(v[:, sx : sx + 4].reshape(256, 128).astype(BF))
    left = jnp.concatenate(parts, axis=1)
    for i, p in enumerate(BITS):
        for n, s in enumerate(BITS):
            tap = tap_of(p, s)
            block = jnp.zeros((64, 128), BF) if tap is None else w_ref[tap * 64 : (tap + 1) * 64, :]
            weights[i * 64 : (i + 1) * 64, n * 128 : (n + 1) * 128] = block
    out = lax.dot_general(left, weights[...], NT, preferred_element_type=F32)
    for z in range(8):
        for x in range(4):
            row = z * 32 + x * 8
            for px in range(2):
                for py in range(2):
                    lane = (px * 2 + py) * 128
                    tile = out[row : row + 8, lane : lane + 128]
                    cells[2 * x + px, z, pl.ds(py, 8, stride=2), :] = tile
        out_ref[:, :, z * 128 : (z + 1) * 128] = cells[:, z].astype(BF)


def deep_kernel(scale, got_ref, other_ref, cot_ref, wide_ref, mine_ref, send_ref, grad_ref, tiles, lat):
    half, core = lax.axis_index("zh"), lax.axis_index("c")
    for y in range(8):
        tiles[2 * y + core] = got_ref[y, 0:32, :]
        tiles[2 * y + 1 - core] = other_ref[y]
    hidden = tiles[...].reshape(512, 1024)
    grad = jnp.dot(cot_ref[...], hidden, preferred_element_type=F32) * scale
    place = {}
    for i, p in enumerate(BITS):
        for n, s in enumerate(BITS):
            tap = tap_of(p, s)
            if tap is not None:
                place[tap] = (n * 16, i * 128)
    for h in range(2):
        for q in range(4):
            blocks = []
            for tap in range(q * 7, q * 7 + 7):
                if tap < 27:
                    row, col = place[tap]
                    blocks.append(grad[row + h * 8 : row + h * 8 + 8, col : col + 128])
                else:
                    blocks.append(jnp.zeros((8, 128), F32))
            grad_ref[h * 4 + q] = jnp.concatenate(blocks, axis=1)
    terms = lax.dot_general(wide_ref[...], hidden, NT, preferred_element_type=F32)
    terms = terms.reshape(8, 16, 512)
    lane = lax.broadcasted_iota(jnp.int32, (16, 512), 1)

    def behind(v, by):
        return pltpu.roll(v, by, 1)

    def shift_z(v):
        return jnp.where(lane % 4 > 0, behind(v, 1), 0.0)

    def shift_y(v):
        edge = jnp.where((lane // 32) % 4 > 0, behind(v, 20), 0.0)
        return jnp.where((lane // 4) % 4 > 0, behind(v, 4), edge)

    over_y = []
    for sx in range(2):
        over_z = [terms[sx * 4 + sy * 2] + shift_z(terms[sx * 4 + sy * 2 + 1]) for sy in range(2)]
        over_y.append(over_z[0] + shift_y(over_z[1]))
    inner = (lane // 16) % 2 == 1
    far = behind(over_y[1], 112)
    edge = jnp.where(lane >= 128, far, 0.0)
    lat[:, 0:512] = over_y[0] + jnp.where(inner, behind(over_y[1], 16), edge)
    lat[:, 512:640] = jnp.where(inner[:, :128], 0.0, far[:, :128])
    mine_ref[...] = lat[pl.ds(pl.multiple_of(half * 8, 8), 8), :]
    send_ref[...] = lat[pl.ds(pl.multiple_of((1 - half) * 8, 8), 8), :]


def body(scale, field_tiles, mid_weight, deep_weight, latent_cotangent):
    half = lax.axis_index("zh")
    field = field_tiles.reshape(8, 16, 1024)
    up_x = [(i, i + 4) for i in range(28)]
    up_y = [(i, i + 1) for i in range(31) if i % 4 != 3]
    down_x = [(i + 4, i) for i in range(28)]
    down_y = [(i + 1, i) for i in range(31) if i % 4 != 3]

    from_x = lax.ppermute(field[7], SPACE, up_x)
    table = jnp.concatenate([deep_weight.T, latent_cotangent.reshape(8, 1024)], axis=1)
    table = lax.all_gather(table, ("c", "zh"), axis=0, tiled=True)
    side = jnp.concatenate([from_x[15:16], field[:, 15]], axis=0)
    from_y = lax.ppermute(side, SPACE, up_y)

    back_parts, cot16, wide16 = call(
        spread_kernel,
        (shape((8, 32, 1024), BF), shape((128, 512), BF), shape((128, 1024), BF)),
        [pltpu.VMEM((256, 1024), F32), pltpu.VMEM((16, 32, 256), F32), pltpu.VMEM((8, 32, 1024), BF)],
        (table,),
        "spread",
    )
    pre, send = call(
        first_kernel,
        (shape((256, 128), F32), shape((8, 64, 1024), BF)),
        [pltpu.VMEM((9, 9, 32, 128), F32), pltpu.VMEM((2304, 128), BF)],
        (field, from_x, from_y, mid_weight, back_parts),
        "first",
    )
    got = lax.all_to_all(send, "y", split_axis=0, concat_axis=0, tiled=True)
    other = lax.ppermute(got[:, 0:32], "c", [(0, 1), (1, 0)])

    back, face_x, face_y = call(
        back_kernel,
        (shape((256, 128), BF), shape((64, 128), BF), shape((32, 128), BF)),
        [pltpu.VMEM((256, 128), F32)],
        (got, pre),
        "back",
    )
    back_x = lax.ppermute(face_x, SPACE, down_x)
    face = jnp.concatenate(
        [face_y.reshape(8, 4, 128), back_x.reshape(8, 8, 128)[:, 0:1]], axis=1
    ).reshape(40, 128)
    back_y = lax.ppermute(face, SPACE, down_y)

    lat_mine, lat_send, grad = call(
        lambda *refs: deep_kernel(scale, *refs),
        (shape((8, 640), F32), shape((8, 640), F32), shape((8, 8, 896), F32)),
        [pltpu.VMEM((16, 32, 1024), BF), pltpu.VMEM((16, 640), F32)],
        (got, other, cot16, wide16),
        "deep",
    )
    lat_got = lax.ppermute(lat_send, "zh", [(0, 1), (1, 0)])
    grad = lax.all_to_all(grad, ("zh", "zl"), split_axis=0, concat_axis=0, tiled=True).sum(0)
    grad = lax.all_to_all(
        jnp.broadcast_to(grad[None], (4, 8, 896)), "x", split_axis=0, concat_axis=0, tiled=True
    ).sum(0)
    grad = lax.all_to_all(
        jnp.broadcast_to(grad[None], (4, 8, 896)), "zl", split_axis=0, concat_axis=0, tiled=True
    )
    grad_deep = grad.transpose(1, 0, 2).reshape(8, 3584)[:, :3456].T

    low = jnp.where(half == 0, lat_mine, lat_got)
    high = jnp.where(half == 0, lat_got, lat_mine)
    latent = jnp.concatenate([low[:, :512], high[:, :128] + low[:, 512:], high[:, 128:512]], axis=1)
    latent = latent.astype(BF).reshape(1, 8, 1024)

    grad_tiles = call(
        field_kernel,
        shape((8, 16, 1024), BF),
        [pltpu.VMEM((512, 1024), BF), pltpu.VMEM((8, 8, 16, 128), F32)],
        (back, back_x, back_y, mid_weight),
        "field",
    )
    return latent, grad_tiles.reshape(1, 1, 8, 16, 1024), grad_deep


def solution(mesh):
    fine = Mesh(mesh.devices.reshape(-1, 4, 2, 8, 2), ("x", "zl", "zh", "y", "c"))
    dp = ("x", "zl")
    scale = 1.0 / math.sqrt(mesh.devices.shape[0] * 1024)
    return jax.shard_map(
        lambda *args: body(scale, *args),
        mesh=fine,
        in_specs=(P(dp, SPACE, None, None, None), P(), P(None, SPACE), P(dp, SPACE, None)),
        out_specs=(P(dp, SPACE, None), P(dp, SPACE, None, None, None), P(None, SPACE)),
        check_vma=False,
    )
```

```python
import itertools
import math

import jax
import jax.numpy as jnp
from jax import lax
from jax.experimental import pallas as pl
from jax.experimental.pallas import tpu as pltpu
from jax.sharding import Mesh, PartitionSpec as P

BF = jnp.bfloat16
F32 = jnp.float32
SPACE = ("zh", "y", "c")
BITS = list(itertools.product((0, 1), repeat=3))
NT = (((1,), (1,)), ((), ()))


def tap_of(parity, shift):
    tap = 0
    for p, s in zip(parity, shift):
        if s > p:
            return None
        tap = tap * 3 + (1 if p == 0 else (0 if s else 2))
    return tap


def call(kernel, out_shape, scratch, args, name):
    return pl.pallas_call(
        kernel,
        out_shape=out_shape,
        in_specs=[pl.BlockSpec(memory_space=pltpu.VMEM)] * len(args),
        out_specs=jax.tree.map(lambda _: pl.BlockSpec(memory_space=pltpu.VMEM), out_shape),
        scratch_shapes=scratch,
        compiler_params=pltpu.CompilerParams(vmem_limit_bytes=40 << 20),
        name=name,
    )(*args)


def shape(dims, dtype):
    return jax.ShapeDtypeStruct(dims, dtype)


def cells_order(rows_first):
    fine = lax.broadcasted_iota(jnp.int32, (256, 256), 0 if rows_first else 1)
    flat = lax.broadcasted_iota(jnp.int32, (256, 256), 1 if rows_first else 0)
    px, py, pz = fine // 128, (fine // 64) % 2, (fine // 32) % 2
    hx, hy, hz = (fine // 16) % 2, (fine // 4) % 4, fine % 4
    return (2 * hz + pz) * 32 + (2 * hx + px) * 8 + 2 * hy + py == flat


def spread_kernel(wc_ref, back_ref, cot_ref, wide_ref, shifted, tiles, weights):
    half, core = lax.axis_index("zh"), lax.axis_index("c")
    order = [wc_ref[(n % 2) * 2 + n // 2].astype(F32) for n in range(4)]
    order = jnp.concatenate(order, axis=0)
    cot = order[:, 3456:]
    kernels = order[:, :3456].astype(BF)
    lane = lax.broadcasted_iota(jnp.int32, cot.shape, 1)

    def ahead(v, by):
        return pltpu.roll(v, 1024 - by, 1)

    def shift_z(v):
        return jnp.where(lane % 4 < 3, ahead(v, 1), 0.0)

    def shift_y(v):
        inner = (lane // 4) % 4 < 3
        edge = jnp.where((lane // 32) % 4 < 3, ahead(v, 20), 0.0)
        return jnp.where(inner, ahead(v, 4), edge)

    def shift_x(v):
        inner = (lane // 16) % 2 == 0
        edge = jnp.where(lane // 128 < 7, ahead(v, 112), 0.0)
        return jnp.where(inner, ahead(v, 16), edge)

    for n, (sx, sy, sz) in enumerate(BITS):
        v = cot
        if sz:
            v = shift_z(v)
        if sy:
            v = shift_y(v)
        if sx:
            v = shift_x(v)
        shifted[n * 32 : (n + 1) * 32, :] = v
    mine = shifted[:, pl.ds(pl.multiple_of(half * 512, 512), 512)]
    tiles[...] = mine.T.reshape(16, 32, 256)
    picked = jnp.concatenate([tiles[2 * y + core] for y in range(8)], axis=0).astype(BF)
    zero = jnp.zeros((32, 128), BF)
    for n, s in enumerate(BITS):
        blocks = []
        for p in BITS:
            tap = tap_of(p, s)
            blocks.append(zero if tap is None else kernels[:, tap * 128 : (tap + 1) * 128])
        weights[n] = jnp.concatenate(blocks, axis=1)
    wide = weights[...].reshape(256, 1024)
    back = jnp.dot(picked, wide, preferred_element_type=F32).astype(BF)
    back_ref[...] = back.reshape(8, 32, 1024)
    row = pl.multiple_of(core * 16, 16)
    for n in range(8):
        wide_ref[n * 16 : (n + 1) * 16, :] = weights[n, pl.ds(row, 16), :]
        part = shifted[pl.ds(pl.multiple_of(n * 32 + core * 16, 16), 16), :]
        cot_ref[n * 16 : (n + 1) * 16, :] = jnp.where(half == 0, part[:, :512], part[:, 512:]).astype(BF)


def first_kernel(field_ref, from_x_ref, from_y_ref, w_ref, back_ref, pre_ref, send_ref, cells, weights):
    cells[:, 0] = jnp.zeros((9, 32, 128), F32)
    for z in range(8):
        lanes = slice(z * 128, (z + 1) * 128)
        cells[0, z + 1, 8:24, :] = from_x_ref[:, lanes].astype(F32)
        cells[1:9, z + 1, 8:24, :] = field_ref[:, :, lanes].astype(F32)
        from_y = from_y_ref[:, lanes].astype(F32)
        for i in range(9):
            cells[i, z + 1, 7:8, :] = from_y[i : i + 1]
    for n in range(9):
        weights[n * 256 : n * 256 + 64, :] = jnp.zeros((64, 128), BF)
        weights[n * 256 + 64 : (n + 1) * 256, :] = w_ref[n * 192 : (n + 1) * 192, :]
    pre = jnp.zeros((256, 128), F32)
    for a in range(3):
        for b in range(3):
            rows = [
                jnp.concatenate(
                    [cells[2 * ox + a, z, pl.ds(7 + b, 8, stride=2), :] for ox in range(4)], axis=0
                )
                for z in range(9)
            ]
            lower, upper = (jnp.concatenate(rows[i : i + 8], axis=0) for i in range(2))
            patch = jnp.concatenate([lower, upper], axis=1).astype(BF)
            n = a * 3 + b
            pre += jnp.dot(patch, weights[n * 256 : (n + 1) * 256, :], preferred_element_type=F32)
    order = cells_order(True).astype(F32)
    pre = jnp.dot(order, pre, precision=lax.Precision.HIGHEST, preferred_element_type=F32)
    pre_ref[...] = pre
    hidden = (pre * (1.0 / (1.0 + jnp.exp(-pre)))).astype(BF)
    hidden = jnp.concatenate([hidden[n * 32 : (n + 1) * 32] for n in range(8)], axis=1)
    for y in range(8):
        send_ref[y, 0:32, :] = hidden
        send_ref[y, 32:64, :] = back_ref[y]


def back_kernel(got_ref, pre_ref, back_ref, face_x_ref, face_y_ref, rows):
    total = got_ref[0, 32:64, :].astype(F32)
    for y in range(1, 8):
        total += got_ref[y, 32:64, :].astype(F32)
    total = jnp.concatenate([total[:, n * 128 : (n + 1) * 128] for n in range(8)], axis=0)
    pre = pre_ref[...]
    gate = 1.0 / (1.0 + jnp.exp(-pre))
    back = (total * gate * (1.0 + pre * (1.0 - gate))).astype(BF)
    order = cells_order(False).astype(F32).astype(BF)
    back = jnp.dot(order, back, preferred_element_type=F32)
    rows[...] = back
    back_ref[...] = back.astype(BF)
    face_x_ref[...] = jnp.concatenate([back[z * 32 : z * 32 + 8] for z in range(8)], axis=0).astype(BF)
    face_y_ref[...] = rows[pl.ds(0, 32, stride=8), :].astype(BF)


def field_kernel(back_ref, from_x_ref, from_y_ref, w_ref, out_ref, weights, cells):
    own = back_ref[...].astype(F32).reshape(8, 4, 8, 128)
    flat = jnp.concatenate([own, from_x_ref[...].astype(F32).reshape(8, 1, 8, 128)], axis=1)
    edge = from_y_ref[...].astype(F32).reshape(40, 1, 128)
    moved = pltpu.roll(flat.reshape(40, 8, 128), 7, 1)
    last = lax.broadcasted_iota(jnp.int32, (40, 8, 128), 1) == 7
    moved = jnp.where(last, jnp.broadcast_to(edge, (40, 8, 128)), moved).reshape(8, 5, 8, 128)
    none = jnp.zeros((1, 5, 8, 128), F32)
    parts = []
    for sx, sy, sz in BITS:
        v = moved if sy else flat
        if sz:
            v = jnp.concatenate([v[1:], none], axis=0)
        parts.append(v[:, sx : sx + 4].reshape(256, 128).astype(BF))
    left = jnp.concatenate(parts, axis=1)
    for i, p in enumerate(BITS):
        for n, s in enumerate(BITS):
            tap = tap_of(p, s)
            block = jnp.zeros((64, 128), BF) if tap is None else w_ref[tap * 64 : (tap + 1) * 64, :]
            weights[i * 64 : (i + 1) * 64, n * 128 : (n + 1) * 128] = block
    out = lax.dot_general(left, weights[...], NT, preferred_element_type=F32)
    for z in range(8):
        for x in range(4):
            row = z * 32 + x * 8
            for px in range(2):
                for py in range(2):
                    lane = (px * 2 + py) * 128
                    tile = out[row : row + 8, lane : lane + 128]
                    cells[2 * x + px, z, pl.ds(py, 8, stride=2), :] = tile
        out_ref[:, :, z * 128 : (z + 1) * 128] = cells[:, z].astype(BF)


def deep_kernel(scale, got_ref, other_ref, cot_ref, wide_ref, mine_ref, send_ref, grad_ref, tiles, lat):
    half, core = lax.axis_index("zh"), lax.axis_index("c")
    for y in range(8):
        tiles[2 * y + core] = got_ref[y, 0:32, :]
        tiles[2 * y + 1 - core] = other_ref[y]
    hidden = tiles[...].reshape(512, 1024)
    grad = jnp.dot(cot_ref[...], hidden, preferred_element_type=F32) * scale
    place = {}
    for i, p in enumerate(BITS):
        for n, s in enumerate(BITS):
            tap = tap_of(p, s)
            if tap is not None:
                place[tap] = (n * 16, i * 128)
    for h in range(2):
        for q in range(4):
            blocks = []
            for tap in range(q * 7, q * 7 + 7):
                if tap < 27:
                    row, col = place[tap]
                    blocks.append(grad[row + h * 8 : row + h * 8 + 8, col : col + 128])
                else:
                    blocks.append(jnp.zeros((8, 128), F32))
            grad_ref[h * 4 + q] = jnp.concatenate(blocks, axis=1)
    terms = lax.dot_general(wide_ref[...], hidden, NT, preferred_element_type=F32)
    terms = terms.reshape(8, 16, 512)
    lane = lax.broadcasted_iota(jnp.int32, (16, 512), 1)

    def behind(v, by):
        return pltpu.roll(v, by, 1)

    def shift_z(v):
        return jnp.where(lane % 4 > 0, behind(v, 1), 0.0)

    def shift_y(v):
        edge = jnp.where((lane // 32) % 4 > 0, behind(v, 20), 0.0)
        return jnp.where((lane // 4) % 4 > 0, behind(v, 4), edge)

    over_y = []
    for sx in range(2):
        over_z = [terms[sx * 4 + sy * 2] + shift_z(terms[sx * 4 + sy * 2 + 1]) for sy in range(2)]
        over_y.append(over_z[0] + shift_y(over_z[1]))
    inner = (lane // 16) % 2 == 1
    far = behind(over_y[1], 112)
    edge = jnp.where(lane >= 128, far, 0.0)
    lat[:, 0:512] = over_y[0] + jnp.where(inner, behind(over_y[1], 16), edge)
    lat[:, 512:640] = jnp.where(inner[:, :128], 0.0, far[:, :128])
    mine_ref[...] = lat[pl.ds(pl.multiple_of(half * 8, 8), 8), :]
    send_ref[...] = lat[pl.ds(pl.multiple_of((1 - half) * 8, 8), 8), :]


def body(scale, field_tiles, mid_weight, deep_weight, latent_cotangent):
    half = lax.axis_index("zh")
    field = field_tiles.reshape(8, 16, 1024)
    up_x = [(i, i + 4) for i in range(28)]
    up_y = [(i, i + 1) for i in range(31) if i % 4 != 3]
    down_x = [(i + 4, i) for i in range(28)]
    down_y = [(i + 1, i) for i in range(31) if i % 4 != 3]

    from_x = lax.ppermute(field[7], SPACE, up_x)
    table = jnp.concatenate([deep_weight.T, latent_cotangent.reshape(8, 1024)], axis=1)
    table = lax.all_gather(table, ("zh", "c"), axis=0)
    from_x, table = lax.optimization_barrier((from_x, table))
    side = jnp.concatenate([from_x[15:16], field[:, 15]], axis=0)
    from_y = lax.ppermute(side, SPACE, up_y)

    back_parts, cot16, wide16 = call(
        spread_kernel,
        (shape((8, 32, 1024), BF), shape((128, 512), BF), shape((128, 1024), BF)),
        [pltpu.VMEM((256, 1024), F32), pltpu.VMEM((16, 32, 256), F32), pltpu.VMEM((8, 32, 1024), BF)],
        (table,),
        "spread",
    )
    pre, send = call(
        first_kernel,
        (shape((256, 128), F32), shape((8, 64, 1024), BF)),
        [pltpu.VMEM((9, 9, 32, 128), F32), pltpu.VMEM((2304, 128), BF)],
        (field, from_x, from_y, mid_weight, back_parts),
        "first",
    )
    got = lax.all_to_all(send, "y", split_axis=0, concat_axis=0, tiled=True)
    other = lax.ppermute(got[:, 0:32], "c", [(0, 1), (1, 0)])

    back, face_x, face_y = call(
        back_kernel,
        (shape((256, 128), BF), shape((64, 128), BF), shape((32, 128), BF)),
        [pltpu.VMEM((256, 128), F32)],
        (got, pre),
        "back",
    )
    lat_mine, lat_send, grad = call(
        lambda *refs: deep_kernel(scale, *refs),
        (shape((8, 640), F32), shape((8, 640), F32), shape((8, 8, 896), F32)),
        [pltpu.VMEM((16, 32, 1024), BF), pltpu.VMEM((16, 640), F32)],
        (got, other, cot16, wide16),
        "deep",
    )
    face_x, grad, lat_send = lax.optimization_barrier((face_x, grad, lat_send))
    back_x = lax.ppermute(face_x, SPACE, down_x)
    grad = lax.all_to_all(grad, ("zh", "zl"), split_axis=0, concat_axis=0, tiled=True).sum(0)
    grad = jnp.broadcast_to(grad[None], (4, 8, 896))
    back_x, grad = lax.optimization_barrier((back_x, grad))
    face = jnp.concatenate(
        [face_y.reshape(8, 4, 128), back_x.reshape(8, 8, 128)[:, 0:1]], axis=1
    ).reshape(40, 128)
    back_y = lax.ppermute(face, SPACE, down_y)
    grad = lax.all_to_all(grad, "x", split_axis=0, concat_axis=0, tiled=True).sum(0)
    grad = jnp.broadcast_to(grad[None], (4, 8, 896))
    back_y, grad, lat_send = lax.optimization_barrier((back_y, grad, lat_send))
    lat_got = lax.ppermute(lat_send, "zh", [(0, 1), (1, 0)])
    grad = lax.all_to_all(grad, "zl", split_axis=0, concat_axis=0, tiled=True)
    grad_deep = grad.transpose(1, 0, 2).reshape(8, 3584)[:, :3456].T

    low = jnp.where(half == 0, lat_mine, lat_got)
    high = jnp.where(half == 0, lat_got, lat_mine)
    latent = jnp.concatenate([low[:, :512], high[:, :128] + low[:, 512:], high[:, 128:512]], axis=1)
    latent = latent.astype(BF).reshape(1, 8, 1024)

    grad_tiles = call(
        field_kernel,
        shape((8, 16, 1024), BF),
        [pltpu.VMEM((512, 1024), BF), pltpu.VMEM((8, 8, 16, 128), F32)],
        (back, back_x, back_y, mid_weight),
        "field",
    )
    return latent, grad_tiles.reshape(1, 1, 8, 16, 1024), grad_deep


def solution(mesh):
    fine = Mesh(mesh.devices.reshape(-1, 4, 2, 8, 2), ("x", "zl", "zh", "y", "c"))
    dp = ("x", "zl")
    scale = 1.0 / math.sqrt(mesh.devices.shape[0] * 1024)
    return jax.shard_map(
        lambda *args: body(scale, *args),
        mesh=fine,
        in_specs=(P(dp, SPACE, None, None, None), P(), P(None, SPACE), P(dp, SPACE, None)),
        out_specs=(P(dp, SPACE, None), P(dp, SPACE, None, None, None), P(None, SPACE)),
        check_vma=False,
    )
```

```python
import itertools
import math

import jax
import jax.numpy as jnp
from jax import lax
from jax.experimental import pallas as pl
from jax.experimental.pallas import tpu as pltpu
from jax.sharding import Mesh, PartitionSpec as P

BF = jnp.bfloat16
F32 = jnp.float32
SPACE = ("zh", "y", "c")
BITS = list(itertools.product((0, 1), repeat=3))
NT = (((1,), (1,)), ((), ()))


def tap_of(parity, shift):
    tap = 0
    for p, s in zip(parity, shift):
        if s > p:
            return None
        tap = tap * 3 + (1 if p == 0 else (0 if s else 2))
    return tap


def call(kernel, out_shape, scratch, args, name):
    return pl.pallas_call(
        kernel,
        out_shape=out_shape,
        in_specs=[pl.BlockSpec(memory_space=pltpu.VMEM)] * len(args),
        out_specs=jax.tree.map(lambda _: pl.BlockSpec(memory_space=pltpu.VMEM), out_shape),
        scratch_shapes=scratch,
        compiler_params=pltpu.CompilerParams(vmem_limit_bytes=40 << 20),
        name=name,
    )(*args)


def shape(dims, dtype):
    return jax.ShapeDtypeStruct(dims, dtype)


def cells_order(rows_first):
    fine = lax.broadcasted_iota(jnp.int32, (256, 256), 0 if rows_first else 1)
    flat = lax.broadcasted_iota(jnp.int32, (256, 256), 1 if rows_first else 0)
    px, py, pz = fine // 128, (fine // 64) % 2, (fine // 32) % 2
    hx, hy, hz = (fine // 16) % 2, (fine // 4) % 4, fine % 4
    return (2 * hz + pz) * 32 + (2 * hx + px) * 8 + 2 * hy + py == flat


def spread_kernel(pair_ref, other_ref, back_ref, cot_ref, wide_ref, tables, shifted, tiles, weights):
    half, core = lax.axis_index("zh"), lax.axis_index("c")
    tables[core * 2 + half] = pair_ref[0].astype(F32)
    tables[core * 2 + 1 - half] = pair_ref[1].astype(F32)
    tables[2 - core * 2 + half] = other_ref[0].astype(F32)
    tables[3 - core * 2 - half] = other_ref[1].astype(F32)
    order = tables[...].reshape(32, 4480)
    cot = order[:, 3456:]
    kernels = order[:, :3456].astype(BF)
    lane = lax.broadcasted_iota(jnp.int32, cot.shape, 1)

    def ahead(v, by):
        return pltpu.roll(v, 1024 - by, 1)

    def shift_z(v):
        return jnp.where(lane % 4 < 3, ahead(v, 1), 0.0)

    def shift_y(v):
        inner = (lane // 4) % 4 < 3
        edge = jnp.where((lane // 32) % 4 < 3, ahead(v, 20), 0.0)
        return jnp.where(inner, ahead(v, 4), edge)

    def shift_x(v):
        inner = (lane // 16) % 2 == 0
        edge = jnp.where(lane // 128 < 7, ahead(v, 112), 0.0)
        return jnp.where(inner, ahead(v, 16), edge)

    for n, (sx, sy, sz) in enumerate(BITS):
        v = cot
        if sz:
            v = shift_z(v)
        if sy:
            v = shift_y(v)
        if sx:
            v = shift_x(v)
        shifted[n * 32 : (n + 1) * 32, :] = v
    mine = shifted[:, pl.ds(pl.multiple_of(half * 512, 512), 512)]
    tiles[...] = mine.T.reshape(16, 32, 256)
    picked = jnp.concatenate([tiles[2 * y + core] for y in range(8)], axis=0).astype(BF)
    zero = jnp.zeros((32, 128), BF)
    for n, s in enumerate(BITS):
        blocks = []
        for p in BITS:
            tap = tap_of(p, s)
            blocks.append(zero if tap is None else kernels[:, tap * 128 : (tap + 1) * 128])
        weights[n] = jnp.concatenate(blocks, axis=1)
    wide = weights[...].reshape(256, 1024)
    back = jnp.dot(picked, wide, preferred_element_type=F32).astype(BF)
    back_ref[...] = back.reshape(8, 32, 1024)
    row = pl.multiple_of(core * 16, 16)
    for n in range(8):
        wide_ref[n * 16 : (n + 1) * 16, :] = weights[n, pl.ds(row, 16), :]
        part = shifted[pl.ds(pl.multiple_of(n * 32 + core * 16, 16), 16), :]
        cot_ref[n * 16 : (n + 1) * 16, :] = jnp.where(half == 0, part[:, :512], part[:, 512:]).astype(BF)


def first_kernel(field_ref, from_x_ref, from_y_ref, w_ref, back_ref, pre_ref, send_ref, cells, weights):
    cells[:, 0] = jnp.zeros((9, 32, 128), F32)
    for z in range(8):
        lanes = slice(z * 128, (z + 1) * 128)
        cells[0, z + 1, 8:24, :] = from_x_ref[:, lanes].astype(F32)
        cells[1:9, z + 1, 8:24, :] = field_ref[:, :, lanes].astype(F32)
        from_y = from_y_ref[:, lanes].astype(F32)
        for i in range(9):
            cells[i, z + 1, 7:8, :] = from_y[i : i + 1]
    for n in range(9):
        weights[n * 256 : n * 256 + 64, :] = jnp.zeros((64, 128), BF)
        weights[n * 256 + 64 : (n + 1) * 256, :] = w_ref[n * 192 : (n + 1) * 192, :]
    pre = jnp.zeros((256, 128), F32)
    for a in range(3):
        for b in range(3):
            rows = [
                jnp.concatenate(
                    [cells[2 * ox + a, z, pl.ds(7 + b, 8, stride=2), :] for ox in range(4)], axis=0
                )
                for z in range(9)
            ]
            lower, upper = (jnp.concatenate(rows[i : i + 8], axis=0) for i in range(2))
            patch = jnp.concatenate([lower, upper], axis=1).astype(BF)
            n = a * 3 + b
            pre += jnp.dot(patch, weights[n * 256 : (n + 1) * 256, :], preferred_element_type=F32)
    order = cells_order(True).astype(F32)
    pre = jnp.dot(order, pre, precision=lax.Precision.HIGHEST, preferred_element_type=F32)
    pre_ref[...] = pre
    hidden = (pre * (1.0 / (1.0 + jnp.exp(-pre)))).astype(BF)
    hidden = jnp.concatenate([hidden[n * 32 : (n + 1) * 32] for n in range(8)], axis=1)
    for y in range(8):
        send_ref[y, 0:32, :] = hidden
        send_ref[y, 32:64, :] = back_ref[y]


def back_kernel(got_ref, pre_ref, back_ref, face_x_ref, face_y_ref, rows):
    total = got_ref[0, 32:64, :].astype(F32)
    for y in range(1, 8):
        total += got_ref[y, 32:64, :].astype(F32)
    total = jnp.concatenate([total[:, n * 128 : (n + 1) * 128] for n in range(8)], axis=0)
    pre = pre_ref[...]
    gate = 1.0 / (1.0 + jnp.exp(-pre))
    back = (total * gate * (1.0 + pre * (1.0 - gate))).astype(BF)
    order = cells_order(False).astype(F32).astype(BF)
    back = jnp.dot(order, back, preferred_element_type=F32)
    rows[...] = back
    back_ref[...] = back.astype(BF)
    face_x_ref[...] = jnp.concatenate([back[z * 32 : z * 32 + 8] for z in range(8)], axis=0).astype(BF)
    face_y_ref[...] = rows[pl.ds(0, 32, stride=8), :].astype(BF)


def field_kernel(back_ref, from_x_ref, from_y_ref, w_ref, out_ref, weights, cells):
    own = back_ref[...].astype(F32).reshape(8, 4, 8, 128)
    flat = jnp.concatenate([own, from_x_ref[...].astype(F32).reshape(8, 1, 8, 128)], axis=1)
    edge = from_y_ref[...].astype(F32).reshape(40, 1, 128)
    moved = pltpu.roll(flat.reshape(40, 8, 128), 7, 1)
    last = lax.broadcasted_iota(jnp.int32, (40, 8, 128), 1) == 7
    moved = jnp.where(last, jnp.broadcast_to(edge, (40, 8, 128)), moved).reshape(8, 5, 8, 128)
    none = jnp.zeros((1, 5, 8, 128), F32)
    parts = []
    for sx, sy, sz in BITS:
        v = moved if sy else flat
        if sz:
            v = jnp.concatenate([v[1:], none], axis=0)
        parts.append(v[:, sx : sx + 4].reshape(256, 128).astype(BF))
    left = jnp.concatenate(parts, axis=1)
    for i, p in enumerate(BITS):
        for n, s in enumerate(BITS):
            tap = tap_of(p, s)
            block = jnp.zeros((64, 128), BF) if tap is None else w_ref[tap * 64 : (tap + 1) * 64, :]
            weights[i * 64 : (i + 1) * 64, n * 128 : (n + 1) * 128] = block
    out = lax.dot_general(left, weights[...], NT, preferred_element_type=F32)
    for z in range(8):
        for x in range(4):
            row = z * 32 + x * 8
            for px in range(2):
                for py in range(2):
                    lane = (px * 2 + py) * 128
                    tile = out[row : row + 8, lane : lane + 128]
                    cells[2 * x + px, z, pl.ds(py, 8, stride=2), :] = tile
        out_ref[:, :, z * 128 : (z + 1) * 128] = cells[:, z].astype(BF)


def deep_kernel(scale, got_ref, other_ref, cot_ref, wide_ref, mine_ref, send_ref, tiles, lat):
    half, core = lax.axis_index("zh"), lax.axis_index("c")
    for y in range(8):
        tiles[2 * y + core] = got_ref[y, 0:32, :]
        tiles[2 * y + 1 - core] = other_ref[y]
    hidden = tiles[...].reshape(512, 1024)
    grad = jnp.dot(cot_ref[...], hidden, preferred_element_type=F32) * scale
    place = {}
    for i, p in enumerate(BITS):
        for n, s in enumerate(BITS):
            tap = tap_of(p, s)
            if tap is not None:
                place[tap] = (n * 16, i * 128)
    terms = lax.dot_general(wide_ref[...], hidden, NT, preferred_element_type=F32)
    terms = terms.reshape(8, 16, 512)
    lane = lax.broadcasted_iota(jnp.int32, (16, 512), 1)

    def behind(v, by):
        return pltpu.roll(v, by, 1)

    def shift_z(v):
        return jnp.where(lane % 4 > 0, behind(v, 1), 0.0)

    def shift_y(v):
        edge = jnp.where((lane // 32) % 4 > 0, behind(v, 20), 0.0)
        return jnp.where((lane // 4) % 4 > 0, behind(v, 4), edge)

    over_y = []
    for sx in range(2):
        over_z = [terms[sx * 4 + sy * 2] + shift_z(terms[sx * 4 + sy * 2 + 1]) for sy in range(2)]
        over_y.append(over_z[0] + shift_y(over_z[1]))
    inner = (lane // 16) % 2 == 1
    far = behind(over_y[1], 112)
    edge = jnp.where(lane >= 128, far, 0.0)
    lat[:, 0:512] = over_y[0] + jnp.where(inner, behind(over_y[1], 16), edge)
    lat[:, 512:640] = jnp.where(inner[:, :128], 0.0, far[:, :128])
    mine_ref[...] = lat[pl.ds(pl.multiple_of(half * 8, 8), 8), :]
    for h in range(2):
        for q in range(4):
            blocks = []
            for tap in range(q * 7, q * 7 + 7):
                if tap < 27:
                    row, col = place[tap]
                    blocks.append(grad[row + h * 8 : row + h * 8 + 8, col : col + 128])
                else:
                    blocks.append(jnp.zeros((8, 128), F32))
            blocks.append(lat[h * 8 : h * 8 + 8, :])
            send_ref[h * 4 + q] = jnp.concatenate(blocks, axis=1).astype(BF)


def middle_kernel(got_ref, mine_ref, send_ref, latent_ref):
    half, place = lax.axis_index("zh"), lax.axis_index("zl")
    total = got_ref[0, :, :896].astype(F32)
    for n in range(1, 8):
        total += got_ref[n, :, :896].astype(F32)
    total = total.astype(BF)
    for n in range(send_ref.shape[0]):
        send_ref[n] = total
    mine = mine_ref[...]
    other = got_ref[(1 - half) * 4 + place][:, 896:].astype(F32)
    low = jnp.where(half == 0, mine, other)
    high = jnp.where(half == 0, other, mine)
    latent_ref[:, 0:512] = low[:, :512].astype(BF)
    latent_ref[:, 512:640] = (high[:, :128] + low[:, 512:]).astype(BF)
    latent_ref[:, 640:1024] = high[:, 128:512].astype(BF)


def last_kernel(got_ref, grad_ref):
    for q in range(4):
        total = got_ref[q].astype(F32)
        for n in range(q + 4, got_ref.shape[0], 4):
            total += got_ref[n].astype(F32)
        width = min(3456 - q * 896, 896)
        grad_ref[:, q * 896 : q * 896 + width] = total[:, :width]


def body(scale, field_tiles, mid_weight, deep_weight, latent_cotangent):
    field = field_tiles.reshape(8, 16, 1024)
    up_x = [(i, i + 4) for i in range(28)]
    up_y = [(i, i + 1) for i in range(31) if i % 4 != 3]
    down_x = [(i + 4, i) for i in range(28)]
    down_y = [(i + 1, i) for i in range(31) if i % 4 != 3]

    swap = [(0, 1), (1, 0)]
    from_x = lax.ppermute(field[7], SPACE, up_x)
    table = jnp.concatenate([deep_weight.T, latent_cotangent.reshape(8, 1024)], axis=1)
    far = lax.ppermute(table, "zh", swap)
    side = jnp.concatenate([from_x[15:16], field[:, 15]], axis=0)
    from_y = lax.ppermute(side, SPACE, up_y)
    pair = jnp.stack([table, far])
    beside = lax.ppermute(pair, "c", swap)

    back_parts, cot16, wide16 = call(
        spread_kernel,
        (shape((8, 32, 1024), BF), shape((128, 512), BF), shape((128, 1024), BF)),
        [
            pltpu.VMEM((4, 8, 4480), F32),
            pltpu.VMEM((256, 1024), F32),
            pltpu.VMEM((16, 32, 256), F32),
            pltpu.VMEM((8, 32, 1024), BF),
        ],
        (pair, beside),
        "spread",
    )
    pre, send = call(
        first_kernel,
        (shape((256, 128), F32), shape((8, 64, 1024), BF)),
        [pltpu.VMEM((9, 9, 32, 128), F32), pltpu.VMEM((2304, 128), BF)],
        (field, from_x, from_y, mid_weight, back_parts),
        "first",
    )
    got = lax.all_to_all(send, "y", split_axis=0, concat_axis=0, tiled=True)
    other = lax.ppermute(got[:, 0:32], "c", swap)

    back, face_x, face_y = call(
        back_kernel,
        (shape((256, 128), BF), shape((64, 128), BF), shape((32, 128), BF)),
        [pltpu.VMEM((256, 128), F32)],
        (got, pre),
        "back",
    )
    lat_mine, grad = call(
        lambda *refs: deep_kernel(scale, *refs),
        (shape((8, 640), F32), shape((8, 8, 1536), BF)),
        [pltpu.VMEM((16, 32, 1024), BF), pltpu.VMEM((16, 640), F32)],
        (got, other, cot16, wide16),
        "deep",
    )
    face_x, grad = lax.optimization_barrier((face_x, grad))
    back_x = lax.ppermute(face_x, SPACE, down_x)
    grad = lax.all_to_all(grad, ("zh", "zl"), split_axis=0, concat_axis=0, tiled=True)
    back_x, grad = lax.optimization_barrier((back_x, grad))
    face = jnp.concatenate(
        [face_y.reshape(8, 4, 128), back_x.reshape(8, 8, 128)[:, 0:1]], axis=1
    ).reshape(40, 128)
    members = lax.axis_size("x") * 4
    grad, latent = call(
        middle_kernel,
        (shape((members, 8, 896), BF), shape((8, 1024), BF)),
        [],
        (grad, lat_mine),
        "middle",
    )
    back_y = lax.ppermute(face, SPACE, down_y)
    grad = lax.all_to_all(grad, ("x", "zl"), split_axis=0, concat_axis=0, tiled=True)
    grad_deep = call(last_kernel, shape((8, 3456), F32), [], (grad,), "last").T
    grad_tiles = call(
        field_kernel,
        shape((8, 16, 1024), BF),
        [pltpu.VMEM((512, 1024), BF), pltpu.VMEM((8, 8, 16, 128), F32)],
        (back, back_x, back_y, mid_weight),
        "field",
    )
    return latent.reshape(1, 8, 1024), grad_tiles.reshape(1, 1, 8, 16, 1024), grad_deep


def solution(mesh):
    fine = Mesh(mesh.devices.reshape(-1, 4, 2, 8, 2), ("x", "zl", "zh", "y", "c"))
    dp = ("x", "zl")
    scale = 1.0 / math.sqrt(mesh.devices.shape[0] * 1024)
    return jax.shard_map(
        lambda *args: body(scale, *args),
        mesh=fine,
        in_specs=(P(dp, SPACE, None, None, None), P(), P(None, SPACE), P(dp, SPACE, None)),
        out_specs=(P(dp, SPACE, None), P(dp, SPACE, None, None, None), P(None, SPACE)),
        check_vma=False,
    )
```

```python
import itertools
import math

import jax
import jax.numpy as jnp
from jax import lax
from jax.experimental import pallas as pl
from jax.experimental.pallas import tpu as pltpu
from jax.sharding import Mesh, PartitionSpec as P

BF = jnp.bfloat16
F32 = jnp.float32
SPACE = ("zh", "y", "c")
BITS = list(itertools.product((0, 1), repeat=3))
NT = (((1,), (1,)), ((), ()))


def tap_of(parity, shift):
    tap = 0
    for p, s in zip(parity, shift):
        if s > p:
            return None
        tap = tap * 3 + (1 if p == 0 else (0 if s else 2))
    return tap


def call(kernel, out_shape, scratch, args, name):
    return pl.pallas_call(
        kernel,
        out_shape=out_shape,
        in_specs=[pl.BlockSpec(memory_space=pltpu.VMEM)] * len(args),
        out_specs=jax.tree.map(lambda _: pl.BlockSpec(memory_space=pltpu.VMEM), out_shape),
        scratch_shapes=scratch,
        compiler_params=pltpu.CompilerParams(vmem_limit_bytes=40 << 20),
        name=name,
    )(*args)


def shape(dims, dtype):
    return jax.ShapeDtypeStruct(dims, dtype)


def cells_order(rows_first):
    fine = lax.broadcasted_iota(jnp.int32, (256, 256), 0 if rows_first else 1)
    flat = lax.broadcasted_iota(jnp.int32, (256, 256), 1 if rows_first else 0)
    px, py, pz = fine // 128, (fine // 64) % 2, (fine // 32) % 2
    hx, hy, hz = (fine // 16) % 2, (fine // 4) % 4, fine % 4
    return (2 * hz + pz) * 32 + (2 * hx + px) * 8 + 2 * hy + py == flat


def spread_kernel(pair_ref, other_ref, back_ref, cot_ref, wide_ref, tables, shifted, tiles, weights):
    half, core = lax.axis_index("zh"), lax.axis_index("c")
    tables[core * 2 + half] = pair_ref[0].astype(F32)
    tables[core * 2 + 1 - half] = pair_ref[1].astype(F32)
    tables[2 - core * 2 + half] = other_ref[0].astype(F32)
    tables[3 - core * 2 - half] = other_ref[1].astype(F32)
    order = tables[...].reshape(32, 4480)
    cot = order[:, 3456:]
    kernels = order[:, :3456].astype(BF)
    lane = lax.broadcasted_iota(jnp.int32, cot.shape, 1)

    def ahead(v, by):
        return pltpu.roll(v, 1024 - by, 1)

    def shift_z(v):
        return jnp.where(lane % 4 < 3, ahead(v, 1), 0.0)

    def shift_y(v):
        inner = (lane // 4) % 4 < 3
        edge = jnp.where((lane // 32) % 4 < 3, ahead(v, 20), 0.0)
        return jnp.where(inner, ahead(v, 4), edge)

    def shift_x(v):
        inner = (lane // 16) % 2 == 0
        edge = jnp.where(lane // 128 < 7, ahead(v, 112), 0.0)
        return jnp.where(inner, ahead(v, 16), edge)

    for n, (sx, sy, sz) in enumerate(BITS):
        v = cot
        if sz:
            v = shift_z(v)
        if sy:
            v = shift_y(v)
        if sx:
            v = shift_x(v)
        shifted[n * 32 : (n + 1) * 32, :] = v
    mine = shifted[:, pl.ds(pl.multiple_of(half * 512, 512), 512)]
    tiles[...] = mine.T.reshape(16, 32, 256)
    picked = jnp.concatenate([tiles[2 * y + core] for y in range(8)], axis=0).astype(BF)
    zero = jnp.zeros((32, 128), BF)
    for n, s in enumerate(BITS):
        blocks = []
        for p in BITS:
            tap = tap_of(p, s)
            blocks.append(zero if tap is None else kernels[:, tap * 128 : (tap + 1) * 128])
        weights[n] = jnp.concatenate(blocks, axis=1)
    wide = weights[...].reshape(256, 1024)
    back = jnp.dot(picked, wide, preferred_element_type=F32).astype(BF)
    back_ref[...] = back.reshape(8, 32, 1024)
    row = pl.multiple_of(core * 16, 16)
    for n in range(8):
        wide_ref[n * 16 : (n + 1) * 16, :] = weights[n, pl.ds(row, 16), :]
        part = shifted[pl.ds(pl.multiple_of(n * 32 + core * 16, 16), 16), :]
        cot_ref[n * 16 : (n + 1) * 16, :] = jnp.where(half == 0, part[:, :512], part[:, 512:]).astype(BF)


def first_kernel(field_ref, from_x_ref, from_y_ref, w_ref, back_ref, pre_ref, send_ref, cells, weights):
    cells[:, 0] = jnp.zeros((9, 32, 128), F32)
    for z in range(8):
        lanes = slice(z * 128, (z + 1) * 128)
        cells[0, z + 1, 8:24, :] = from_x_ref[:, lanes].astype(F32)
        cells[1:9, z + 1, 8:24, :] = field_ref[:, :, lanes].astype(F32)
        from_y = from_y_ref[:, lanes].astype(F32)
        for i in range(9):
            cells[i, z + 1, 7:8, :] = from_y[i : i + 1]
    for n in range(9):
        weights[n * 256 : n * 256 + 64, :] = jnp.zeros((64, 128), BF)
        weights[n * 256 + 64 : (n + 1) * 256, :] = w_ref[n * 192 : (n + 1) * 192, :]
    pre = jnp.zeros((256, 128), F32)
    for a in range(3):
        for b in range(3):
            rows = [
                jnp.concatenate(
                    [cells[2 * ox + a, z, pl.ds(7 + b, 8, stride=2), :] for ox in range(4)], axis=0
                )
                for z in range(9)
            ]
            lower, upper = (jnp.concatenate(rows[i : i + 8], axis=0) for i in range(2))
            patch = jnp.concatenate([lower, upper], axis=1).astype(BF)
            n = a * 3 + b
            pre += jnp.dot(patch, weights[n * 256 : (n + 1) * 256, :], preferred_element_type=F32)
    order = cells_order(True).astype(F32)
    pre = jnp.dot(order, pre, precision=lax.Precision.HIGHEST, preferred_element_type=F32)
    pre_ref[...] = pre
    hidden = (pre * (1.0 / (1.0 + jnp.exp(-pre)))).astype(BF)
    hidden = jnp.concatenate([hidden[n * 32 : (n + 1) * 32] for n in range(8)], axis=1)
    for y in range(8):
        send_ref[y, 0:32, :] = hidden
        send_ref[y, 32:64, :] = back_ref[y]


def back_kernel(got_ref, pre_ref, back_ref, face_x_ref, face_y_ref, rows):
    total = got_ref[0, 32:64, :].astype(F32)
    for y in range(1, 8):
        total += got_ref[y, 32:64, :].astype(F32)
    total = jnp.concatenate([total[:, n * 128 : (n + 1) * 128] for n in range(8)], axis=0)
    pre = pre_ref[...]
    gate = 1.0 / (1.0 + jnp.exp(-pre))
    back = (total * gate * (1.0 + pre * (1.0 - gate))).astype(BF)
    order = cells_order(False).astype(F32).astype(BF)
    back = jnp.dot(order, back, preferred_element_type=F32)
    rows[...] = back
    back_ref[...] = back.astype(BF)
    face_x_ref[...] = jnp.concatenate([back[z * 32 : z * 32 + 8] for z in range(8)], axis=0).astype(BF)
    face_y_ref[...] = rows[pl.ds(0, 32, stride=8), :].astype(BF)


def field_kernel(back_ref, from_x_ref, from_y_ref, w_ref, out_ref, weights, cells):
    own = back_ref[...].astype(F32).reshape(8, 4, 8, 128)
    from_x = from_x_ref[...].astype(F32)
    flat = jnp.concatenate([own, from_x[:64].reshape(8, 1, 8, 128)], axis=1)
    edge = from_y_ref[...].astype(F32).reshape(8, 4, 1, 128)
    edge = jnp.concatenate([edge, from_x[64:72].reshape(8, 1, 1, 128)], axis=1).reshape(40, 1, 128)
    moved = pltpu.roll(flat.reshape(40, 8, 128), 7, 1)
    last = lax.broadcasted_iota(jnp.int32, (40, 8, 128), 1) == 7
    moved = jnp.where(last, jnp.broadcast_to(edge, (40, 8, 128)), moved).reshape(8, 5, 8, 128)
    none = jnp.zeros((1, 5, 8, 128), F32)
    parts = []
    for sx, sy, sz in BITS:
        v = moved if sy else flat
        if sz:
            v = jnp.concatenate([v[1:], none], axis=0)
        parts.append(v[:, sx : sx + 4].reshape(256, 128).astype(BF))
    left = jnp.concatenate(parts, axis=1)
    for i, p in enumerate(BITS):
        for n, s in enumerate(BITS):
            tap = tap_of(p, s)
            block = jnp.zeros((64, 128), BF) if tap is None else w_ref[tap * 64 : (tap + 1) * 64, :]
            weights[i * 64 : (i + 1) * 64, n * 128 : (n + 1) * 128] = block
    out = lax.dot_general(left, weights[...], NT, preferred_element_type=F32)
    for z in range(8):
        for x in range(4):
            row = z * 32 + x * 8
            for px in range(2):
                for py in range(2):
                    lane = (px * 2 + py) * 128
                    tile = out[row : row + 8, lane : lane + 128]
                    cells[2 * x + px, z, pl.ds(py, 8, stride=2), :] = tile
        out_ref[:, :, z * 128 : (z + 1) * 128] = cells[:, z].astype(BF)


def deep_kernel(scale, got_ref, other_ref, cot_ref, wide_ref, mine_ref, send_ref, tiles, lat):
    half, core = lax.axis_index("zh"), lax.axis_index("c")
    for y in range(8):
        tiles[2 * y + core] = got_ref[y, 0:32, :]
        tiles[2 * y + 1 - core] = other_ref[y]
    hidden = tiles[...].reshape(512, 1024)
    grad = jnp.dot(cot_ref[...], hidden, preferred_element_type=F32) * scale
    place = {}
    for i, p in enumerate(BITS):
        for n, s in enumerate(BITS):
            tap = tap_of(p, s)
            if tap is not None:
                place[tap] = (n * 16, i * 128)
    terms = lax.dot_general(wide_ref[...], hidden, NT, preferred_element_type=F32)
    terms = terms.reshape(8, 16, 512)
    lane = lax.broadcasted_iota(jnp.int32, (16, 512), 1)

    def behind(v, by):
        return pltpu.roll(v, by, 1)

    def shift_z(v):
        return jnp.where(lane % 4 > 0, behind(v, 1), 0.0)

    def shift_y(v):
        edge = jnp.where((lane // 32) % 4 > 0, behind(v, 20), 0.0)
        return jnp.where((lane // 4) % 4 > 0, behind(v, 4), edge)

    over_y = []
    for sx in range(2):
        over_z = [terms[sx * 4 + sy * 2] + shift_z(terms[sx * 4 + sy * 2 + 1]) for sy in range(2)]
        over_y.append(over_z[0] + shift_y(over_z[1]))
    inner = (lane // 16) % 2 == 1
    far = behind(over_y[1], 112)
    edge = jnp.where(lane >= 128, far, 0.0)
    lat[:, 0:512] = over_y[0] + jnp.where(inner, behind(over_y[1], 16), edge)
    lat[:, 512:640] = jnp.where(inner[:, :128], 0.0, far[:, :128])
    mine_ref[...] = lat[pl.ds(pl.multiple_of(half * 8, 8), 8), :]
    for h in range(2):
        for q in range(4):
            blocks = []
            for tap in range(q * 7, q * 7 + 7):
                if tap < 27:
                    row, col = place[tap]
                    blocks.append(grad[row + h * 8 : row + h * 8 + 8, col : col + 128])
                else:
                    blocks.append(jnp.zeros((8, 128), F32))
            blocks.append(lat[h * 8 : h * 8 + 8, :])
            send_ref[q * 2 + h] = jnp.concatenate(blocks, axis=1).astype(BF)


def middle_kernel(got_ref, mine_ref, send_ref, latent_ref):
    half, place = lax.axis_index("zh"), lax.axis_index("zl")
    total = got_ref[0, :, :896].astype(F32)
    for n in range(1, 8):
        total += got_ref[n, :, :896].astype(F32)
    total = total.astype(BF)
    for n in range(send_ref.shape[0]):
        send_ref[n] = total
    mine = mine_ref[...]
    other = got_ref[place * 2 + 1 - half][:, 896:].astype(F32)
    low = jnp.where(half == 0, mine, other)
    high = jnp.where(half == 0, other, mine)
    latent_ref[:, 0:512] = low[:, :512].astype(BF)
    latent_ref[:, 512:640] = (high[:, :128] + low[:, 512:]).astype(BF)
    latent_ref[:, 640:1024] = high[:, 128:512].astype(BF)


def last_kernel(got_ref, grad_ref):
    for q in range(4):
        total = got_ref[q].astype(F32)
        for n in range(q + 4, got_ref.shape[0], 4):
            total += got_ref[n].astype(F32)
        width = min(3456 - q * 896, 896)
        grad_ref[:, q * 896 : q * 896 + width] = total[:, :width]


def body(scale, field_tiles, mid_weight, deep_weight, latent_cotangent):
    field = field_tiles.reshape(8, 16, 1024)
    up_x = [(i, i + 4) for i in range(28)]
    up_y = [(i, i + 1) for i in range(31) if i % 4 != 3]
    down_x = [(i + 4, i) for i in range(28)]
    down_y = [(i + 1, i) for i in range(31) if i % 4 != 3]

    swap = [(0, 1), (1, 0)]
    from_x = lax.ppermute(field[7], SPACE, up_x)
    table = jnp.concatenate([deep_weight.T, latent_cotangent.reshape(8, 1024)], axis=1)
    far = lax.ppermute(table, "zh", swap)
    side = jnp.concatenate([from_x[15:16], field[:, 15]], axis=0)
    from_y = lax.ppermute(side, SPACE, up_y)
    pair = jnp.stack([table, far])
    beside = lax.ppermute(pair, "c", swap)

    back_parts, cot16, wide16 = call(
        spread_kernel,
        (shape((8, 32, 1024), BF), shape((128, 512), BF), shape((128, 1024), BF)),
        [
            pltpu.VMEM((4, 8, 4480), F32),
            pltpu.VMEM((256, 1024), F32),
            pltpu.VMEM((16, 32, 256), F32),
            pltpu.VMEM((8, 32, 1024), BF),
        ],
        (pair, beside),
        "spread",
    )
    pre, send = call(
        first_kernel,
        (shape((256, 128), F32), shape((8, 64, 1024), BF)),
        [pltpu.VMEM((9, 9, 32, 128), F32), pltpu.VMEM((2304, 128), BF)],
        (field, from_x, from_y, mid_weight, back_parts),
        "first",
    )
    got = lax.all_to_all(send, "y", split_axis=0, concat_axis=0, tiled=True)
    other = lax.ppermute(got[:, 0:32], "c", swap)

    back, face_x, face_y = call(
        back_kernel,
        (shape((256, 128), BF), shape((64, 128), BF), shape((32, 128), BF)),
        [pltpu.VMEM((256, 128), F32)],
        (got, pre),
        "back",
    )
    lat_mine, grad = call(
        lambda *refs: deep_kernel(scale, *refs),
        (shape((8, 640), F32), shape((8, 8, 1536), BF)),
        [pltpu.VMEM((16, 32, 1024), BF), pltpu.VMEM((16, 640), F32)],
        (got, other, cot16, wide16),
        "deep",
    )
    face_y, grad = lax.optimization_barrier((face_y, grad))
    back_y = lax.ppermute(face_y, SPACE, down_y)
    grad = lax.all_to_all(grad, ("zl", "zh"), split_axis=0, concat_axis=0, tiled=True)
    back_y, grad = lax.optimization_barrier((back_y, grad))
    corner = back_y.reshape(8, 4, 128)[:, 0]
    face = jnp.concatenate([face_x, corner, corner], axis=0)
    members = lax.axis_size("x") * 4
    grad, latent = call(
        middle_kernel,
        (shape((members, 8, 896), BF), shape((8, 1024), BF)),
        [],
        (grad, lat_mine),
        "middle",
    )
    back_x = lax.ppermute(face, SPACE, down_x)
    grad = lax.all_to_all(grad, ("x", "zl"), split_axis=0, concat_axis=0, tiled=True)
    grad_deep = call(last_kernel, shape((8, 3456), F32), [], (grad,), "last").T
    grad_tiles = call(
        field_kernel,
        shape((8, 16, 1024), BF),
        [pltpu.VMEM((512, 1024), BF), pltpu.VMEM((8, 8, 16, 128), F32)],
        (back, back_x, back_y, mid_weight),
        "field",
    )
    return latent.reshape(1, 8, 1024), grad_tiles.reshape(1, 1, 8, 16, 1024), grad_deep


def solution(mesh):
    fine = Mesh(mesh.devices.reshape(-1, 4, 2, 8, 2), ("x", "zl", "zh", "y", "c"))
    dp = ("x", "zl")
    scale = 1.0 / math.sqrt(mesh.devices.shape[0] * 1024)
    return jax.shard_map(
        lambda *args: body(scale, *args),
        mesh=fine,
        in_specs=(P(dp, SPACE, None, None, None), P(), P(None, SPACE), P(dp, SPACE, None)),
        out_specs=(P(dp, SPACE, None), P(dp, SPACE, None, None, None), P(None, SPACE)),
        check_vma=False,
    )
```

```python
import itertools
import math

import jax
import jax.numpy as jnp
from jax import lax
from jax.experimental import pallas as pl
from jax.experimental.pallas import tpu as pltpu
from jax.sharding import Mesh, PartitionSpec as P

BF = jnp.bfloat16
F32 = jnp.float32
SPACE = ("zh", "y", "c")
BITS = list(itertools.product((0, 1), repeat=3))
NT = (((1,), (1,)), ((), ()))


def tap_of(parity, shift):
    tap = 0
    for p, s in zip(parity, shift):
        if s > p:
            return None
        tap = tap * 3 + (1 if p == 0 else (0 if s else 2))
    return tap


def call(kernel, out_shape, scratch, args, name):
    return pl.pallas_call(
        kernel,
        out_shape=out_shape,
        in_specs=[pl.BlockSpec(memory_space=pltpu.VMEM)] * len(args),
        out_specs=jax.tree.map(lambda _: pl.BlockSpec(memory_space=pltpu.VMEM), out_shape),
        scratch_shapes=scratch,
        compiler_params=pltpu.CompilerParams(vmem_limit_bytes=40 << 20),
        name=name,
    )(*args)


def shape(dims, dtype):
    return jax.ShapeDtypeStruct(dims, dtype)


def cells_order(rows_first):
    fine = lax.broadcasted_iota(jnp.int32, (256, 256), 0 if rows_first else 1)
    flat = lax.broadcasted_iota(jnp.int32, (256, 256), 1 if rows_first else 0)
    px, py, pz = fine // 128, (fine // 64) % 2, (fine // 32) % 2
    hx, hy, hz = (fine // 16) % 2, (fine // 4) % 4, fine % 4
    return (2 * hz + pz) * 32 + (2 * hx + px) * 8 + 2 * hy + py == flat


def spread_kernel(pair_ref, other_ref, back_ref, cot_ref, wide_ref, tables, shifted, tiles, weights):
    half, core = lax.axis_index("zh"), lax.axis_index("c")
    tables[core * 2 + half] = pair_ref[0].astype(F32)
    tables[core * 2 + 1 - half] = pair_ref[1].astype(F32)
    tables[2 - core * 2 + half] = other_ref[0].astype(F32)
    tables[3 - core * 2 - half] = other_ref[1].astype(F32)
    order = tables[...].reshape(32, 4480)
    cot = order[:, 3456:]
    kernels = order[:, :3456].astype(BF)
    lane = lax.broadcasted_iota(jnp.int32, cot.shape, 1)

    def ahead(v, by):
        return pltpu.roll(v, 1024 - by, 1)

    def shift_z(v):
        return jnp.where(lane % 4 < 3, ahead(v, 1), 0.0)

    def shift_y(v):
        inner = (lane // 4) % 4 < 3
        edge = jnp.where((lane // 32) % 4 < 3, ahead(v, 20), 0.0)
        return jnp.where(inner, ahead(v, 4), edge)

    def shift_x(v):
        inner = (lane // 16) % 2 == 0
        edge = jnp.where(lane // 128 < 7, ahead(v, 112), 0.0)
        return jnp.where(inner, ahead(v, 16), edge)

    for n, (sx, sy, sz) in enumerate(BITS):
        v = cot
        if sz:
            v = shift_z(v)
        if sy:
            v = shift_y(v)
        if sx:
            v = shift_x(v)
        shifted[n * 32 : (n + 1) * 32, :] = v
    mine = shifted[:, pl.ds(pl.multiple_of(half * 512, 512), 512)]
    tiles[...] = mine.T.reshape(16, 32, 256)
    picked = jnp.concatenate([tiles[2 * y + core] for y in range(8)], axis=0).astype(BF)
    zero = jnp.zeros((32, 128), BF)
    for n, s in enumerate(BITS):
        blocks = []
        for p in BITS:
            tap = tap_of(p, s)
            blocks.append(zero if tap is None else kernels[:, tap * 128 : (tap + 1) * 128])
        weights[n] = jnp.concatenate(blocks, axis=1)
    wide = weights[...].reshape(256, 1024)
    back = jnp.dot(picked, wide, preferred_element_type=F32).astype(BF)
    back_ref[...] = back.reshape(8, 32, 1024)
    row = pl.multiple_of(core * 16, 16)
    for n in range(8):
        wide_ref[n * 16 : (n + 1) * 16, :] = weights[n, pl.ds(row, 16), :]
        part = shifted[pl.ds(pl.multiple_of(n * 32 + core * 16, 16), 16), :]
        cot_ref[n * 16 : (n + 1) * 16, :] = jnp.where(half == 0, part[:, :512], part[:, 512:]).astype(BF)


def first_kernel(field_ref, from_x_ref, from_y_ref, w_ref, back_ref, pre_ref, send_ref, cells, weights):
    cells[:, 0] = jnp.zeros((9, 32, 128), F32)
    for z in range(8):
        lanes = slice(z * 128, (z + 1) * 128)
        cells[0, z + 1, 8:24, :] = from_x_ref[:, lanes].astype(F32)
        cells[1:9, z + 1, 8:24, :] = field_ref[:, :, lanes].astype(F32)
        from_y = from_y_ref[:, lanes].astype(F32)
        for i in range(9):
            cells[i, z + 1, 7:8, :] = from_y[i : i + 1]
    for n in range(9):
        weights[n * 256 : n * 256 + 64, :] = jnp.zeros((64, 128), BF)
        weights[n * 256 + 64 : (n + 1) * 256, :] = w_ref[n * 192 : (n + 1) * 192, :]
    pre = jnp.zeros((256, 128), F32)
    for a in range(3):
        for b in range(3):
            rows = [
                jnp.concatenate(
                    [cells[2 * ox + a, z, pl.ds(7 + b, 8, stride=2), :] for ox in range(4)], axis=0
                )
                for z in range(9)
            ]
            lower, upper = (jnp.concatenate(rows[i : i + 8], axis=0) for i in range(2))
            patch = jnp.concatenate([lower, upper], axis=1).astype(BF)
            n = a * 3 + b
            pre += jnp.dot(patch, weights[n * 256 : (n + 1) * 256, :], preferred_element_type=F32)
    order = cells_order(True).astype(F32)
    pre = jnp.dot(order, pre, precision=lax.Precision.HIGHEST, preferred_element_type=F32)
    pre_ref[...] = pre
    hidden = (pre * (1.0 / (1.0 + jnp.exp(-pre)))).astype(BF)
    hidden = jnp.concatenate([hidden[n * 32 : (n + 1) * 32] for n in range(8)], axis=1)
    for y in range(8):
        send_ref[y, 0:32, :] = hidden
        send_ref[y, 32:64, :] = back_ref[y]


def back_kernel(got_ref, pre_ref, back_ref, face_x_ref, face_y_ref, rows):
    total = got_ref[0, 32:64, :].astype(F32)
    for y in range(1, 8):
        total += got_ref[y, 32:64, :].astype(F32)
    total = jnp.concatenate([total[:, n * 128 : (n + 1) * 128] for n in range(8)], axis=0)
    pre = pre_ref[...]
    gate = 1.0 / (1.0 + jnp.exp(-pre))
    back = (total * gate * (1.0 + pre * (1.0 - gate))).astype(BF)
    order = cells_order(False).astype(F32).astype(BF)
    back = jnp.dot(order, back, preferred_element_type=F32)
    rows[...] = back
    back_ref[...] = back.astype(BF)
    face_x_ref[...] = jnp.concatenate([back[z * 32 : z * 32 + 8] for z in range(8)], axis=0).astype(BF)
    face_y_ref[...] = rows[pl.ds(0, 32, stride=8), :].astype(BF)


def field_kernel(back_ref, from_x_ref, from_y_ref, w_ref, out_ref, weights, cells):
    own = back_ref[...].astype(F32).reshape(8, 4, 8, 128)
    flat = jnp.concatenate([own, from_x_ref[...].astype(F32).reshape(8, 1, 8, 128)], axis=1)
    edge = from_y_ref[...].astype(F32).reshape(40, 1, 128)
    moved = pltpu.roll(flat.reshape(40, 8, 128), 7, 1)
    last = lax.broadcasted_iota(jnp.int32, (40, 8, 128), 1) == 7
    moved = jnp.where(last, jnp.broadcast_to(edge, (40, 8, 128)), moved).reshape(8, 5, 8, 128)
    none = jnp.zeros((1, 5, 8, 128), F32)
    parts = []
    for sx, sy, sz in BITS:
        v = moved if sy else flat
        if sz:
            v = jnp.concatenate([v[1:], none], axis=0)
        parts.append(v[:, sx : sx + 4].reshape(256, 128).astype(BF))
    left = jnp.concatenate(parts, axis=1)
    for i, p in enumerate(BITS):
        for n, s in enumerate(BITS):
            tap = tap_of(p, s)
            block = jnp.zeros((64, 128), BF) if tap is None else w_ref[tap * 64 : (tap + 1) * 64, :]
            weights[i * 64 : (i + 1) * 64, n * 128 : (n + 1) * 128] = block
    out = lax.dot_general(left, weights[...], NT, preferred_element_type=F32)
    for z in range(8):
        for x in range(4):
            row = z * 32 + x * 8
            for px in range(2):
                for py in range(2):
                    lane = (px * 2 + py) * 128
                    tile = out[row : row + 8, lane : lane + 128]
                    cells[2 * x + px, z, pl.ds(py, 8, stride=2), :] = tile
        out_ref[:, :, z * 128 : (z + 1) * 128] = cells[:, z].astype(BF)


def deep_kernel(scale, got_ref, other_ref, cot_ref, wide_ref, mine_ref, send_ref, tiles, lat):
    half, core = lax.axis_index("zh"), lax.axis_index("c")
    for y in range(8):
        tiles[2 * y + core] = got_ref[y, 0:32, :]
        tiles[2 * y + 1 - core] = other_ref[y]
    hidden = tiles[...].reshape(512, 1024)
    grad = jnp.dot(cot_ref[...], hidden, preferred_element_type=F32) * scale
    place = {}
    for i, p in enumerate(BITS):
        for n, s in enumerate(BITS):
            tap = tap_of(p, s)
            if tap is not None:
                place[tap] = (n * 16, i * 128)
    terms = lax.dot_general(wide_ref[...], hidden, NT, preferred_element_type=F32)
    terms = terms.reshape(8, 16, 512)
    lane = lax.broadcasted_iota(jnp.int32, (16, 512), 1)

    def behind(v, by):
        return pltpu.roll(v, by, 1)

    def shift_z(v):
        return jnp.where(lane % 4 > 0, behind(v, 1), 0.0)

    def shift_y(v):
        edge = jnp.where((lane // 32) % 4 > 0, behind(v, 20), 0.0)
        return jnp.where((lane // 4) % 4 > 0, behind(v, 4), edge)

    over_y = []
    for sx in range(2):
        over_z = [terms[sx * 4 + sy * 2] + shift_z(terms[sx * 4 + sy * 2 + 1]) for sy in range(2)]
        over_y.append(over_z[0] + shift_y(over_z[1]))
    inner = (lane // 16) % 2 == 1
    far = behind(over_y[1], 112)
    edge = jnp.where(lane >= 128, far, 0.0)
    lat[:, 0:512] = over_y[0] + jnp.where(inner, behind(over_y[1], 16), edge)
    lat[:, 512:640] = jnp.where(inner[:, :128], 0.0, far[:, :128])
    mine_ref[...] = lat[pl.ds(pl.multiple_of(half * 8, 8), 8), :]
    for h in range(2):
        for q in range(4):
            blocks = []
            for tap in range(q * 7, q * 7 + 7):
                if tap < 27:
                    row, col = place[tap]
                    blocks.append(grad[row + h * 8 : row + h * 8 + 8, col : col + 128])
                else:
                    blocks.append(jnp.zeros((8, 128), F32))
            blocks.append(lat[h * 8 : h * 8 + 8, :])
            send_ref[q * 2 + h] = jnp.concatenate(blocks, axis=1).astype(BF)


def middle_kernel(got_ref, mine_ref, send_ref, latent_ref):
    half, place = lax.axis_index("zh"), lax.axis_index("zl")
    total = got_ref[0, :, :896].astype(F32)
    for n in range(1, 8):
        total += got_ref[n, :, :896].astype(F32)
    total = total.astype(BF)
    for n in range(send_ref.shape[0]):
        send_ref[n] = total
    mine = mine_ref[...]
    other = got_ref[place * 2 + 1 - half][:, 896:].astype(F32)
    low = jnp.where(half == 0, mine, other)
    high = jnp.where(half == 0, other, mine)
    latent_ref[:, 0:512] = low[:, :512].astype(BF)
    latent_ref[:, 512:640] = (high[:, :128] + low[:, 512:]).astype(BF)
    latent_ref[:, 640:1024] = high[:, 128:512].astype(BF)


def last_kernel(got_ref, grad_ref):
    for q in range(4):
        total = got_ref[q].astype(F32)
        for n in range(q + 4, got_ref.shape[0], 4):
            total += got_ref[n].astype(F32)
        width = min(3456 - q * 896, 896)
        grad_ref[:, q * 896 : q * 896 + width] = total[:, :width]


def body(scale, field_tiles, mid_weight, deep_weight, latent_cotangent):
    field = field_tiles.reshape(8, 16, 1024)
    up_x = [(i, i + 4) for i in range(28)]
    up_y = [(i, i + 1) for i in range(31) if i % 4 != 3]
    down_x = [(i + 4, i) for i in range(28)]
    down_y = [(i + 1, i) for i in range(31) if i % 4 != 3]

    swap = [(0, 1), (1, 0)]
    from_x = lax.ppermute(field[7], SPACE, up_x)
    table = jnp.concatenate([deep_weight.T, latent_cotangent.reshape(8, 1024)], axis=1)
    far = lax.ppermute(table, "zh", swap)
    side = jnp.concatenate([from_x[15:16], field[:, 15]], axis=0)
    from_y = lax.ppermute(side, SPACE, up_y)
    pair = jnp.stack([table, far])
    beside = lax.ppermute(pair, "c", swap)

    back_parts, cot16, wide16 = call(
        spread_kernel,
        (shape((8, 32, 1024), BF), shape((128, 512), BF), shape((128, 1024), BF)),
        [
            pltpu.VMEM((4, 8, 4480), F32),
            pltpu.VMEM((256, 1024), F32),
            pltpu.VMEM((16, 32, 256), F32),
            pltpu.VMEM((8, 32, 1024), BF),
        ],
        (pair, beside),
        "spread",
    )
    pre, send = call(
        first_kernel,
        (shape((256, 128), F32), shape((8, 64, 1024), BF)),
        [pltpu.VMEM((9, 9, 32, 128), F32), pltpu.VMEM((2304, 128), BF)],
        (field, from_x, from_y, mid_weight, back_parts),
        "first",
    )
    got = lax.all_to_all(send, "y", split_axis=0, concat_axis=0, tiled=True)
    other = lax.ppermute(got[:, 0:32], "c", swap)

    back, face_x, face_y = call(
        back_kernel,
        (shape((256, 128), BF), shape((64, 128), BF), shape((32, 128), BF)),
        [pltpu.VMEM((256, 128), F32)],
        (got, pre),
        "back",
    )
    lat_mine, grad = call(
        lambda *refs: deep_kernel(scale, *refs),
        (shape((8, 640), F32), shape((8, 8, 1536), BF)),
        [pltpu.VMEM((16, 32, 1024), BF), pltpu.VMEM((16, 640), F32)],
        (got, other, cot16, wide16),
        "deep",
    )
    face_x, grad = lax.optimization_barrier((face_x, grad))
    back_x = lax.ppermute(face_x, SPACE, down_x)
    grad = lax.all_to_all(grad, ("zl", "zh"), split_axis=0, concat_axis=0, tiled=True)
    back_x, grad = lax.optimization_barrier((back_x, grad))
    face = jnp.concatenate(
        [face_y.reshape(8, 4, 128), back_x.reshape(8, 8, 128)[:, 0:1]], axis=1
    ).reshape(40, 128)
    members = lax.axis_size("x") * 4
    grad, latent = call(
        middle_kernel,
        (shape((members, 8, 896), BF), shape((8, 1024), BF)),
        [],
        (grad, lat_mine),
        "middle",
    )
    back_y = lax.ppermute(face, SPACE, down_y)
    grad = lax.all_to_all(grad, ("x", "zl"), split_axis=0, concat_axis=0, tiled=True)
    grad_deep = call(last_kernel, shape((8, 3456), F32), [], (grad,), "last").T
    grad_tiles = call(
        field_kernel,
        shape((8, 16, 1024), BF),
        [pltpu.VMEM((512, 1024), BF), pltpu.VMEM((8, 8, 16, 128), F32)],
        (back, back_x, back_y, mid_weight),
        "field",
    )
    return latent.reshape(1, 8, 1024), grad_tiles.reshape(1, 1, 8, 16, 1024), grad_deep


def solution(mesh):
    fine = Mesh(mesh.devices.reshape(-1, 4, 2, 8, 2), ("x", "zl", "zh", "y", "c"))
    dp = ("x", "zl")
    scale = 1.0 / math.sqrt(mesh.devices.shape[0] * 1024)
    return jax.shard_map(
        lambda *args: body(scale, *args),
        mesh=fine,
        in_specs=(P(dp, SPACE, None, None, None), P(), P(None, SPACE), P(dp, SPACE, None)),
        out_specs=(P(dp, SPACE, None), P(dp, SPACE, None, None, None), P(None, SPACE)),
        check_vma=False,
    )
```
